128 devices in a mesh: head: 4 (over x), seq: 32 (over z, y, core).
Axes of the slice: x: 4, y: 4, z: 4, core: 2. Of those that a mesh axis runs over, the one named last changes fastest.
Arguments:
- acts: bfloat16 [32768, 1664], P('seq'), may hold values from -40 to 40
- w_qkv: bfloat16 [3, 1664, 1664], P(None, None, 'head'), may hold values from -1 to 1
- w_out: bfloat16 [1664, 1664], P('head'), may hold values from -0.15625 to 0.15625
- gain: float32 [1664], replicated, may hold values from 0.4 to 1.6
- w_merge: bfloat16 [6656, 1664], P('head'), may hold values from -0.078125 to 0.078125
- seg_ids: int32 [8192], replicated, may hold values from 0 to 63, never falling along the last dimension, each value on 1 to 256 neighbouring positions
- pad_mask: int32 [32768], replicated, may hold values 0 or 1
- owners: int32 [8192, 1], P('seq'), may hold values from 0 to 31; in each aligned block of 256 rows (0 to 255, 256 to 511, ...) at most 16 rows name the same one
Outputs:
- routed: bfloat16 [16384, 1664], P('seq', 'head')
The draws below stay inside these ranges and needn't reach their ends.
Inputs may be any that keep to these rules, and one draw needn't show every extreme that they name: `seg_ids`: Non-decreasing; each image covers 1 to 256 consecutive windows. `owners`: among the 256 windows of one device, at most 16 name the same owner.
All inputs are finite; a program needn't handle non-finite values.
Results may differ from the reference program's by a relative error of at most 0.0085.
Values may be sent and summed in bfloat16 or wider, within the bound.
A program may use at most 256 MiB of HBM per device.

```python
import math
import jax
import jax.numpy as jnp
import numpy as np
from jax import lax

D = 1664
HEADS = 16
HEAD_DIM = 104
TOK_DEV = 1024
TOKENS = 32768
MERGED = 8192
WIN_DEV = 256
SEG_MOST = 256
SEGS = 64
CAP = 16
N_SEQ = 32


def draw_acts(key, part):
    key_base = jax.random.fold_in(key, 11)
    values = jnp.clip(jax.random.normal(key_base, (TOKENS, D), jnp.float32), -6.0, 6.0)
    return values.astype(jnp.bfloat16)


def draw_w_qkv(key, part):
    first = jax.random.normal(jax.random.fold_in(key, 21), (D, D), jnp.float32) * D ** (-0.5)
    second = jax.random.normal(jax.random.fold_in(key, 22), (D, D), jnp.float32) * D ** (-0.5)
    third = jax.random.normal(jax.random.fold_in(key, 23), (D, D), jnp.float32) * D ** (-0.5)
    stacked = jnp.stack([first, second, third])
    return jnp.clip(stacked, -1.0, 1.0).astype(jnp.bfloat16)


def place_ends(drawn, rng, least, top_value):
    longest = drawn.shape.index(max(drawn.shape))
    spots = []
    for shift in (0, 1):
        where = [jax.random.randint(jax.random.fold_in(rng, axis), (), 0, length) for axis, length in enumerate(drawn.shape)]
        where[longest] = (where[longest] + shift) % drawn.shape[longest]
        spots.append(tuple(where))
    return drawn.at[spots[0]].set(least).at[spots[1]].set(top_value)


def levels(rng, shape, pieces, low, high):
    level = 1.0
    for position, parts in pieces:
        heights = jax.random.uniform(jax.random.fold_in(jax.random.fold_in(rng, 6), position), (parts,), jnp.float32, low / len(pieces), high / len(pieces))
        level = level * jnp.repeat(jnp.exp(heights), shape[position] // parts).reshape((-1,) + (1,) * (len(shape) - 1 - position))
    return level


def length_profile(number_of, total, bound, slope):
    portions = [(1 << 20) // math.isqrt(grade ** slope) + 1 for grade in range(2, number_of + 1)]
    rest, holding = total - bound - (number_of - 1), [1] * (number_of - 1)
    while rest > 0:
        movable = [i for i in range(number_of - 1) if holding[i] < bound]
        whole, budget = sum([portions[i] for i in movable]), rest
        for i in movable:
            more = min(bound - holding[i], max(1, budget * portions[i] // whole), rest)
            holding[i] = holding[i] + more
            rest = rest - more
    return np.array([bound] + holding)


def ragged(rng, number_of, total, most, slope):
    if number_of == 2:
        one = jax.random.randint(rng, (), max(1, total - most), min(most, total - 1) + 1)
        return jnp.stack([one, total - one])
    sizes = jnp.asarray(length_profile(number_of, total, most, slope), jnp.int32)
    couples = (number_of - 1) // 2
    donor, sink = sizes[1:1 + 2 * couples:2], sizes[2:2 + 2 * couples:2]
    slack = jnp.minimum(donor - 1, most - sink)
    moved = jax.random.randint(jax.random.fold_in(rng, 1), (couples,), 0, 1 << 20) % (slack + 1)
    sizes = sizes.at[1:1 + 2 * couples:2].set(donor - moved).at[2:2 + 2 * couples:2].set(sink + moved)
    return sizes[jax.random.permutation(jax.random.fold_in(rng, 2), number_of)]


def routed_block(key, own, number, rows, count, top, limit, slope):
    order = jax.random.permutation(key, count)
    crowded, usual = shares(count, rows * top, limit, slope, True), shares(count, rows * top, limit, slope, False)
    places = jnp.arange(count)

    def named(lengths, rotation):
        used = int((lengths > 0).sum())
        fixed = max(1, used // 4)
        moved = fixed + (places - fixed + rotation * (used - fixed)) % max(1, count - fixed)
        return jnp.zeros((count,), jnp.int32).at[order[jnp.where(places < fixed, places, moved)]].set(jnp.asarray(lengths, jnp.int32))

    lengths = jnp.where(number % 4 == 0, named(crowded, number // 4), named(usual, number - number // 4 - 1))
    mixed = jax.random.permutation(jax.random.fold_in(own, 3), count)
    source_of, sink = mixed[0:count // 2 * 2:2], mixed[1:count // 2 * 2:2]
    margin = jnp.minimum(lengths[source_of] - 1, limit - lengths[sink]) // 2
    margin = jnp.where((source_of == order[0]) | (sink == order[0]) | (lengths[sink] == 0), 0, jnp.maximum(margin, 0))
    moved = jax.random.randint(jax.random.fold_in(own, 4), (count // 2,), 0, 1 << 20) % (margin + 1)
    lengths = lengths.at[source_of].add(-moved).at[sink].add(moved)
    labels = jnp.searchsorted(jnp.cumsum(lengths), jnp.arange(rows * top), side="right").astype(jnp.int32)
    listing = labels.reshape(top, rows).T
    listing = listing[jax.random.permutation(jax.random.fold_in(own, 1), rows)]
    rotation = jax.random.randint(jax.random.fold_in(own, 2), (rows, 1), 0, top)
    return jnp.take_along_axis(listing, (jnp.arange(top)[None, :] + rotation) % top, axis=1)


def shares(number_of, total, reach, skew, full):
    loads = [(1 << 20) // math.isqrt(rank ** skew) + 1 for rank in range(1, number_of + 1)]
    largest = reach if full else min(reach, max(-(-total // number_of), total * loads[0] // sum(loads)))
    least = 1 if total - largest >= number_of - 1 else 0
    holding, surplus = [largest] + [least] * (number_of - 1), total - largest - least * (number_of - 1)
    while surplus > 0:
        candidates = [i for i in range(1, number_of) if holding[i] < largest] or [i for i in range(1, number_of) if holding[i] < reach]
        whole, budget = sum([loads[i] for i in candidates]), surplus
        for i in candidates:
            extra = min(reach - holding[i], max(1, budget * loads[i] // whole), surplus)
            holding[i] = holding[i] + extra
            surplus = surplus - extra
    return np.array(holding)


def centred(key, shape, deviation, most, split=(), kind=jnp.bfloat16):
    level = levels(key, shape, split, -0.22, 0.18) if split else 1.0
    values = jax.random.normal(key, shape, jnp.float32) * deviation * level
    return jnp.minimum(jnp.maximum(values, -most), most).astype(kind)


def setup_inputs(seed: int = 0) -> dict:
    keys = jax.random.split(jax.random.key(seed), 9)
    acts = draw_acts(jax.random.fold_in(keys[8], 71), 0)
    w_qkv = draw_w_qkv(jax.random.fold_in(keys[8], 71), 0)
    w_out = centred(keys[2], (D, D), D ** -0.5, 0.15625, ((0, 4),))
    gain = jnp.clip(1.0 + 0.12 * jax.random.normal(keys[3], (D,), jnp.float32), 0.4, 1.6)
    w_merge = centred(keys[4], (4 * D, D), (4 * D) ** -0.5, 0.078125, ((0, 4),))
    seg_ids = jnp.searchsorted(jnp.cumsum(ragged(keys[5], SEGS, MERGED, SEG_MOST, 2)), jnp.arange(MERGED), side="right").astype(jnp.int32)
    pad_mask = place_ends((jax.random.randint(keys[6], (TOKENS,), 0, 8) < 7).astype(jnp.int32), jax.random.fold_in(keys[6], 1), 0, 1)
    owners_keys = jax.random.split(jax.random.fold_in(keys[7], 1), MERGED // WIN_DEV)
    owners_turns = jax.random.permutation(jax.random.fold_in(keys[7], 3), MERGED // WIN_DEV)
    owners = jax.vmap(lambda own, number: routed_block(jax.random.fold_in(keys[7], 2), own, number, WIN_DEV, N_SEQ, 1, CAP, 2))(owners_keys, owners_turns).reshape((MERGED, 1))
    return dict(acts=acts, w_qkv=w_qkv, w_out=w_out, gain=gain, w_merge=w_merge, seg_ids=seg_ids, pad_mask=pad_mask, owners=owners)


def reference(acts, w_qkv, w_out, gain, w_merge, seg_ids, pad_mask, owners):
    projected = jnp.einsum('td,kdh->kth', acts.astype(jnp.float32), w_qkv.astype(jnp.float32)).astype(jnp.bfloat16)
    queries = projected[0]
    filler = jnp.zeros((TOK_DEV, D), jnp.bfloat16)
    keys_padded = jnp.concatenate([filler, projected[1], filler], axis=0)
    values_padded = jnp.concatenate([filler, projected[2], filler], axis=0)
    seg_tokens = jnp.repeat(seg_ids, 4).astype(jnp.int32)
    seg_fill = jnp.full((TOK_DEV,), -1, jnp.int32)
    seg_padded = jnp.concatenate([seg_fill, seg_tokens, seg_fill])
    live_fill = jnp.zeros((TOK_DEV,), jnp.int32)
    live_padded = jnp.concatenate([live_fill, pad_mask, live_fill])
    scale = HEAD_DIM ** (-0.5)

    def one_block(block):
        first = (block * TOK_DEV).astype(jnp.int32)
        qpart = lax.dynamic_slice_in_dim(queries, first, TOK_DEV, 0).astype(jnp.float32).reshape(TOK_DEV, HEADS, HEAD_DIM)
        kpart = lax.dynamic_slice_in_dim(keys_padded, first, 3 * TOK_DEV, 0).astype(jnp.float32).reshape(3 * TOK_DEV, HEADS, HEAD_DIM)
        vpart = lax.dynamic_slice_in_dim(values_padded, first, 3 * TOK_DEV, 0).astype(jnp.float32).reshape(3 * TOK_DEV, HEADS, HEAD_DIM)
        query_img = lax.dynamic_slice_in_dim(seg_tokens, first, TOK_DEV, 0)
        query_live = lax.dynamic_slice_in_dim(pad_mask, first, TOK_DEV, 0)
        key_img = lax.dynamic_slice_in_dim(seg_padded, first, 3 * TOK_DEV, 0)
        key_live = lax.dynamic_slice_in_dim(live_padded, first, 3 * TOK_DEV, 0)
        query_pos = first + jnp.arange(TOK_DEV, dtype=jnp.int32)
        key_pos = first - TOK_DEV + jnp.arange(3 * TOK_DEV, dtype=jnp.int32)
        allowed = (query_img[:, None] == key_img[None, :]) & ((key_live[None, :] == 1) | (query_pos[:, None] == key_pos[None, :]))
        scores = jnp.einsum('qhd,khd->hqk', qpart, kpart) * scale
        masked = jnp.where(allowed[None], scores, -1e+30)
        highest = lax.optimization_barrier(jnp.max(masked, axis=2, keepdims=True))
        weights = jnp.where(allowed[None], jnp.exp(scores - highest), 0.0)
        total = lax.optimization_barrier(jnp.sum(weights, axis=2))
        rounded = lax.optimization_barrier(weights.astype(jnp.bfloat16))
        summed = jnp.einsum('hqk,khd->qhd', rounded.astype(jnp.float32), vpart)
        result = (summed / jnp.transpose(total)[:, :, None]).reshape(TOK_DEV, D)
        return (result * query_live[:, None].astype(jnp.float32)).astype(jnp.bfloat16)
    blocks = TOKENS // TOK_DEV
    attn = lax.map(one_block, jnp.arange(blocks, dtype=jnp.int32)).reshape(TOKENS, D)
    hidden = acts.astype(jnp.float32) + jnp.dot(attn, w_out, preferred_element_type=jnp.float32)
    centre = lax.optimization_barrier(jnp.mean(hidden, axis=1, keepdims=True))
    centered = hidden - centre
    variance = lax.optimization_barrier(jnp.mean(centered * centered, axis=1, keepdims=True))
    normed = (centered * lax.rsqrt(variance + 1e-06) * gain[None, :]).astype(jnp.bfloat16)
    merged = jnp.dot(normed.reshape(MERGED, 4 * D), w_merge, preferred_element_type=jnp.float32).astype(jnp.bfloat16)
    owner = owners[:, 0].astype(jnp.int32)
    hits = (owner[:, None] == jnp.arange(N_SEQ, dtype=jnp.int32)[None, :]).astype(jnp.int32)
    hits = hits.reshape(N_SEQ, WIN_DEV, N_SEQ)
    earlier = jnp.cumsum(hits, axis=1) - 1
    rank = lax.optimization_barrier(jnp.sum(hits * earlier, axis=2)).reshape(MERGED)
    sender = jnp.arange(MERGED, dtype=jnp.int32) // WIN_DEV
    target = owner * (N_SEQ * CAP) + sender * CAP + rank
    routed = jnp.zeros((N_SEQ * N_SEQ * CAP, D), jnp.bfloat16).at[target].set(merged)
    return routed
```

```python
import functools
import math

import jax
import jax.numpy as jnp
from jax import lax
from jax.experimental import pallas as pl
from jax.experimental.pallas import tpu as pltpu
from jax.sharding import PartitionSpec as P

HEAD_DIM = 104
BLK = 256
WIN = BLK // 4
NB = 4
MESH = pl.DeviceIdType.MESH
NEG = -1e30
F32 = jnp.float32
BF16 = jnp.bfloat16
K_OFF = (0, 0, 128, 256)


def iota(shape, dim):
    return lax.broadcasted_iota(jnp.int32, shape, dim)


def nt_dot(a, b):
    return lax.dot_general(a, b, (((1,), (1,)), ((), ())), preferred_element_type=F32)


def nn_dot(a, b):
    return lax.dot_general(a, b, (((1,), (0,)), ((), ())), preferred_element_type=F32)


def kernel(
    n_seq,
    n_head,
    acts_hbm,
    wqkv_hbm,
    wout_hbm,
    gain_ref,
    wmerge_hbm,
    seg_ref,
    pad_ref,
    owner_ref,
    out_hbm,
    acts,
    wst,
    wq,
    wkv,
    kv,
    qm,
    acc,
    mst,
    lst,
    bias,
    wfull,
    wmerge,
    resid,
    asend,
    arecv,
    psend,
    precv,
    outgoing,
    qimg,
    qlive,
    kcode,
    acts_sem,
    wst_sem,
    wl_sem,
    kv_ssem,
    kv_rsem,
    w1_ssem,
    w1_rsem,
    w2_ssem,
    w2_rsem,
    w3_ssem,
    w3_rsem,
    a_ssem,
    a_rsem,
    p_ssem,
    p_rsem,
    o_ssem,
    o_rsem,
    o_lsem,
):
    d = acts.shape[1]
    s = lax.axis_index("seq")
    h = lax.axis_index("head")
    core = lax.rem(s, 2)
    right = lax.rem(s + 1, n_seq)
    left = lax.rem(s + n_seq - 1, n_seq)
    partner = s + 1 - 2 * core
    hp1 = lax.rem(h + 1, n_head)
    hm1 = lax.rem(h + n_head - 1, n_head)
    hp2 = lax.rem(h + 2, n_head)

    def acts_copy(c):
        rows = pl.ds(c * BLK, BLK)
        return pltpu.make_async_copy(acts_hbm.at[rows], acts.at[rows], acts_sem.at[c])

    def wst_copy(k):
        return pltpu.make_async_copy(wqkv_hbm.at[k], wst.at[k], wst_sem.at[k])

    wst_copy(1).start()
    wst_copy(2).start()
    acts_copy(3).start()
    acts_copy(0).start()
    acts_copy(2).start()
    acts_copy(1).start()
    wst_copy(0).start()
    wout_local = pltpu.make_async_copy(wout_hbm, wfull.at[h], wl_sem.at[0])
    wout_local.start()
    wmerge_local = pltpu.make_async_copy(wmerge_hbm, wmerge, wl_sem.at[1])
    wmerge_local.start()

    barrier = pltpu.get_barrier_semaphore()
    for k in range(1, n_head):
        pl.semaphore_signal(
            barrier, inc=1, device_id={"head": lax.rem(h + k, n_head)}, device_id_type=MESH
        )

    def greet(k, carry):
        pl.semaphore_signal(
            barrier, inc=1, device_id={"seq": lax.rem(s + k, n_seq)}, device_id_type=MESH
        )
        return carry

    lax.fori_loop(1, n_seq, greet, 0)

    n_img_rows = seg_ref.shape[0]
    n_pad_rows = pad_ref.shape[0]
    expand = (iota((128, 512), 0) == iota((128, 512), 1) // 4).astype(BF16)
    expand_t = (iota((512, 128), 1) == iota((512, 128), 0) // 4).astype(BF16)
    eye = (iota((128, 128), 0) == iota((128, 128), 1)).astype(BF16)
    for r in range(6):
        row = 2 * s - 2 + r
        inside = jnp.logical_and(row >= 0, row < n_img_rows)
        safe = jnp.clip(row, 0, n_img_rows - 1)
        seg_row = seg_ref[pl.ds(safe, 1), :].astype(F32)
        seg_row = jnp.where(inside, seg_row, -1.0)
        wide = jnp.broadcast_to(seg_row, (128, 128)).astype(BF16)
        codes = nn_dot(wide[:16], expand)[:1]
        if 2 <= r < 4:
            qimg[(r - 2) * 512 : (r - 1) * 512, :] = nt_dot(expand_t, wide)
        for half in range(2):
            chunk = 2 * r + half
            for part in range(2):
                prow = 4 * (2 * s - 2 + r) + 2 * half + part
                pin = jnp.clip(prow, 0, n_pad_rows - 1)
                live = pad_ref[pl.ds(pin, 1), :].astype(F32)
                lanes = slice(half * 256 + part * 128, half * 256 + part * 128 + 128)
                code = jnp.where(jnp.logical_and(inside, live == 1.0), codes[:, lanes], -2.0)
                kcode[chunk : chunk + 1, part * 128 : part * 128 + 128] = code
                if 2 <= r < 4:
                    at = (r - 2) * 512 + half * 256 + part * 128
                    livew = jnp.broadcast_to(live, (128, 128)).astype(BF16)
                    qlive[at : at + 128, :] = nt_dot(eye, livew)

    wst_copy(1).wait()
    wst_copy(2).wait()
    wkv[:, 0:384] = wst[1, :, 0:384]
    wkv[:, 512:896] = wst[2, :, 0:384]
    wkv[:, 384:512] = jnp.concatenate(
        [wst[2, :, 384:416], wst[1, :, 384:416], jnp.zeros((d, 64), BF16)], axis=1
    )

    pl.semaphore_wait(barrier, n_seq - 1 + n_head - 1)

    half_rows = wout_hbm.shape[0] // 2
    q_rows = (half_rows // 32 + 1) * 16
    mine = pl.ds(pl.multiple_of(core * half_rows, 16), half_rows)
    first = pl.ds(pl.multiple_of(core * half_rows, 16), q_rows)
    second = pl.ds(pl.multiple_of(core * half_rows + q_rows, 16), half_rows - q_rows)

    def remote(src, dst, ssem, rsem, dev):
        return pltpu.make_async_remote_copy(
            src_ref=src, dst_ref=dst, send_sem=ssem, recv_sem=rsem, device_id=dev, device_id_type=MESH
        )

    w1 = [
        remote(
            wout_hbm.at[mine], wfull.at[h, mine], w1_ssem.at[0], w1_rsem.at[0], {"head": hp1}
        ),
        remote(
            wout_hbm.at[mine], wfull.at[h, mine], w1_ssem.at[1], w1_rsem.at[1], {"head": hm1}
        ),
    ]
    w1[0].start()
    w1[1].start()

    def halo(t):
        way = lax.rem(t, 2)
        step = t // 2
        c = jnp.where(way == 0, NB - 1 - step, step)
        dst = jnp.where(way == 0, c, 2 * NB + c)
        to = jnp.where(way == 0, right, left)
        return c, remote(
            kv.at[NB + c], kv.at[dst], kv_ssem.at[way, step], kv_rsem.at[way, step], {"seq": to}
        )

    def project_kv(t, carry):
        c, copy = halo(t)
        acts_copy(c).wait()
        rows = pl.ds(pl.multiple_of(c * BLK, BLK), BLK)
        kv[NB + c] = nn_dot(acts[rows, :], wkv[...]).astype(BF16)
        copy.start()
        return carry

    lax.fori_loop(0, NB, project_kv, 0)

    def send_rest(t, carry):
        halo(t)[1].start()
        return carry

    lax.fori_loop(NB, 2 * NB, send_rest, 0)

    wst_copy(0).wait()
    wq[:, 0:384] = wst[0, :, 0:384]
    wq[:, 384:512] = jnp.concatenate(
        [jnp.zeros((d, 32), BF16), wst[0, :, 384:416], jnp.zeros((d, 64), BF16)], axis=1
    )
    scale = math.log2(math.e) / math.sqrt(HEAD_DIM)
    pick = (iota((WIN, BLK), 1) == 4 * iota((WIN, BLK), 0) + h).astype(BF16)

    def slot_of(i):
        return jnp.where(i == 0, 2, jnp.where(i == 3, 3, i - 1))

    def project_q(i, carry):
        rows = pl.ds(pl.multiple_of(i * BLK, BLK), BLK)
        q = nn_dot(acts[rows, :], wq[...]) * scale
        lane = iota((BLK, 512), 1)
        for k in range(4):
            lo, hi = k * HEAD_DIM, (k + 1) * HEAD_DIM if k < 3 else 512
            keep = jnp.where(jnp.logical_and(lane >= lo, lane < hi), q, 0.0)
            qm[k, rows, :] = keep[:, K_OFF[k] : K_OFF[k] + 256].astype(BF16)
        out_rows = pl.ds(pl.multiple_of(slot_of(i) * WIN, WIN), WIN)
        resid[out_rows, :] = nn_dot(pick, acts[rows, :])
        return carry

    lax.fori_loop(0, NB, project_q, 0)

    def values_of(block, k):
        if k < 3:
            off = 512 + K_OFF[k]
            return block[:, off : off + 256]
        return jnp.concatenate([block[:, 768:896], block[:, 384:512]], axis=1)

    def own(i, carry):
        rows = pl.ds(pl.multiple_of(i * BLK, BLK), BLK)
        qi = qimg[rows, :]
        qi = jnp.concatenate([qi, qi], axis=1)
        ahead = iota((BLK, BLK), 1) - iota((BLK, BLK), 0)
        for c in range(NB):
            ok = jnp.logical_or(qi == kcode[NB + c : NB + c + 1, :], ahead == BLK * (i - c))
            bias[:, c * BLK : (c + 1) * BLK] = jnp.where(ok, 0.0, NEG)
        keys = kv[NB : 2 * NB].reshape(NB * BLK, 896)
        for k in range(4):
            sc = nt_dot(qm[k, rows, :], keys[:, K_OFF[k] : K_OFF[k] + 256]) + bias[...]
            m = jnp.max(sc, axis=1, keepdims=True)
            p = jnp.exp2(sc - m)
            total = jnp.sum(p, axis=1, keepdims=True)
            acc[i, k] = nn_dot(p.astype(BF16), values_of(keys, k))
            mst[i, k] = jnp.broadcast_to(m, (BLK, 128))
            lst[i, k] = jnp.broadcast_to(total, (BLK, 128))
        return carry

    lax.fori_loop(0, NB, own, 0)

    w1[0].wait()
    w1[1].wait()
    w2 = [
        remote(
            wfull.at[hm1, first], wfull.at[hm1, first], w2_ssem.at[0], w2_rsem.at[0], {"head": hp1}
        ),
        remote(
            wfull.at[hp1, second], wfull.at[hp1, second], w2_ssem.at[1], w2_rsem.at[1], {"head": hm1}
        ),
    ]
    w3 = [
        remote(wfull.at[src, mine], wfull.at[src, mine], w3_ssem.at[k], w3_rsem.at[k], {"seq": partner})
        for k, src in enumerate((hm1, hp1, hp2))
    ]
    w2[0].start()
    w2[1].start()
    w3[0].start()
    w3[1].start()

    def pair(i, j):
        rows = pl.ds(pl.multiple_of(i * BLK, BLK), BLK)
        qi = qimg[rows, :]
        qi = jnp.concatenate([qi, qi], axis=1)
        off = jnp.where(qi == kcode[pl.ds(j, 1), :], 0.0, NEG)
        keys = kv[j]
        for k in range(4):
            sc = nt_dot(qm[k, rows, :], keys[:, K_OFF[k] : K_OFF[k] + 256]) + off
            m_old = mst[i, k]
            m = jnp.maximum(m_old, jnp.max(sc, axis=1, keepdims=True))
            alpha = jnp.exp2(m_old - m)
            mm = jnp.concatenate([m, m], axis=1)
            p = jnp.exp2(sc - mm)
            lst[i, k] = lst[i, k] * alpha + jnp.sum(p, axis=1, keepdims=True)
            aa = jnp.concatenate([alpha, alpha], axis=1)
            acc[i, k] = acc[i, k] * aa + nn_dot(p.astype(BF16), values_of(keys, k))
            mst[i, k] = m

    def near(t, carry):
        halo(2 * t)[1].wait_recv()
        halo(2 * t + 1)[1].wait_recv()

        def from_left(i, c2):
            pair(i, NB - 1 - t)
            return c2

        def from_right(i, c2):
            pair(i, 2 * NB + t)
            return c2

        lax.fori_loop(0, NB - t, from_left, 0)
        lax.fori_loop(t, NB, from_right, 0)
        return carry

    order = (iota((BLK, BLK), 1) == 4 * (iota((BLK, BLK), 0) % WIN) + iota((BLK, BLK), 0) // WIN).astype(
        BF16
    )

    def attn_copies(i):
        rows = pl.ds(pl.multiple_of(slot_of(i) * WIN, WIN), WIN)
        return [
            remote(
                asend.at[lax.rem(h + k, n_head), rows],
                arecv.at[h, rows],
                a_ssem.at[i, k - 1],
                a_rsem.at[i, k - 1],
                {"head": lax.rem(h + k, n_head)},
            )
            for k in range(1, n_head)
        ]

    def finish(i):
        rows = pl.ds(pl.multiple_of(i * BLK, BLK), BLK)
        live = qlive[rows, :]
        o = []
        for k in range(4):
            inv = live / lst[i, k]
            o.append(acc[i, k] * jnp.concatenate([inv, inv], axis=1))
        lane = iota((BLK, 128), 1)
        t0 = jnp.where(lane < HEAD_DIM, o[0][:, :128], o[1][:, :128])
        t1 = jnp.where(lane + 128 < 2 * HEAD_DIM, o[1][:, 128:], o[2][:, :128])
        t2 = jnp.where(lane + 256 < 3 * HEAD_DIM, o[2][:, 128:], o[3][:, :128])
        full = jnp.concatenate([t0, t1, t2, o[3][:, 128:]], axis=1).astype(BF16)
        sorted_rows = nn_dot(order, full).astype(BF16)
        out_rows = pl.ds(pl.multiple_of(slot_of(i) * WIN, WIN), WIN)
        for p in range(4):
            asend[p, out_rows, :] = sorted_rows[p * WIN : (p + 1) * WIN, :416]
        arecv[h, out_rows, :] = asend[h, out_rows, :]
        for copy in attn_copies(i):
            copy.start()

    def finish_loop(i, carry):
        finish(i)
        return carry

    lax.fori_loop(0, NB - 1, near, 0)
    lax.fori_loop(1, 3, finish_loop, 0)
    w2[0].wait()
    w2[1].wait()
    w3[2].start()
    lax.fori_loop(NB - 1, NB, near, 0)

    def finish_ends(i, carry):
        finish(3 * i)
        return carry

    lax.fori_loop(0, 2, finish_ends, 0)

    wout_local.wait()
    wmerge_local.wait()
    for copy in w3:
        copy.wait()

    def part_copies(t):
        rows = pl.ds(pl.multiple_of(t * 128, 128), 128)
        return [
            remote(
                psend.at[lax.rem(h + k, n_head), rows],
                precv.at[h, rows],
                p_ssem.at[t, k - 1],
                p_rsem.at[t, k - 1],
                {"head": lax.rem(h + k, n_head)},
            )
            for k in range(1, n_head)
        ]

    def tail(t, carry):
        for i in (jnp.where(t == 0, 1, 0), jnp.where(t == 0, 2, 3)):
            for copy in attn_copies(i):
                copy.wait()
        rows = pl.ds(pl.multiple_of(t * 128, 128), 128)
        hidden = resid[rows, :]
        for src in range(4):
            hidden = hidden + nn_dot(arecv[src, rows, :], wfull[src])
        mean = jnp.sum(hidden, axis=1, keepdims=True) * (1.0 / d)
        centered = hidden - mean
        var = jnp.sum(centered * centered, axis=1, keepdims=True) * (1.0 / d)
        normed = (centered * lax.rsqrt(var + 1e-6) * gain_ref[...]).astype(BF16)
        prod = nn_dot(normed, wmerge[...])
        for c in range(4):
            psend[c, rows, :] = prod[:, c * 416 : (c + 1) * 416].astype(BF16)
        precv[h, rows, :] = psend[h, rows, :]
        for copy in part_copies(t):
            copy.start()
        return carry

    lax.fori_loop(0, 2, tail, 0)

    own0 = owner_ref[0:1, :].astype(F32)
    own1 = owner_ref[1:2, :].astype(F32)
    orow = jnp.concatenate([own0, own1], axis=1)
    ocol = jnp.concatenate(
        [
            nt_dot(eye, jnp.broadcast_to(own0, (128, 128)).astype(BF16)),
            nt_dot(eye, jnp.broadcast_to(own1, (128, 128)).astype(BF16)),
        ],
        axis=0,
    )
    ocol = jnp.concatenate([ocol, ocol], axis=1)
    earlier = jnp.logical_and(ocol == orow, iota((256, 256), 0) < iota((256, 256), 1))
    rank = jnp.sum(jnp.where(earlier, 1.0, 0.0), axis=0, keepdims=True)
    cap = 1024 // (2 * n_seq)
    slot = orow * float(cap) + rank
    place = (iota((n_seq * cap, 256), 0).astype(F32) == slot).astype(BF16)

    for t in range(2):
        for copy in part_copies(t):
            copy.wait()
    merged = (
        precv[0].astype(F32) + precv[1].astype(F32) + precv[2].astype(F32) + precv[3].astype(F32)
    ).astype(BF16)
    merged = jnp.concatenate([merged[128:192], merged[0:128], merged[192:256]], axis=0)
    outgoing[...] = nn_dot(place, merged).astype(BF16)

    def route(k):
        to = lax.rem(s + k, n_seq)
        return remote(
            outgoing.at[pl.ds(pl.multiple_of(to * cap, cap), cap)],
            out_hbm.at[pl.ds(pl.multiple_of(s * cap, cap), cap)],
            o_ssem.at[k],
            o_rsem.at[k],
            {"seq": to},
        )

    here = pl.ds(pl.multiple_of(s * cap, cap), cap)
    local = pltpu.make_async_copy(outgoing.at[here], out_hbm.at[here], o_lsem.at[0])
    local.start()

    def route_start(k, carry):
        route(k).start()
        return carry

    def route_wait(k, carry):
        route(k).wait()
        return carry

    def halo_done(t, carry):
        halo(t)[1].wait_send()
        return carry

    lax.fori_loop(1, n_seq, route_start, 0)
    lax.fori_loop(0, 2 * NB, halo_done, 0)
    lax.fori_loop(1, n_seq, route_wait, 0)
    local.wait()


def per_device(n_seq, n_head, acts, w_qkv, w_out, gain, w_merge, seg_ids, pad_mask, owners):
    rows, d = acts.shape
    hidden = w_qkv.shape[2]
    wins = rows // 4
    vmem = pltpu.VMEM
    dma = pltpu.SemaphoreType.DMA
    any_spec = pl.BlockSpec(memory_space=pl.ANY)
    vmem_spec = pl.BlockSpec(memory_space=pltpu.VMEM)
    return pl.pallas_call(
        functools.partial(kernel, n_seq, n_head),
        out_shape=jax.ShapeDtypeStruct((rows // 2, hidden), BF16),
        in_specs=[any_spec, any_spec, any_spec, vmem_spec, any_spec, vmem_spec, vmem_spec, vmem_spec],
        out_specs=any_spec,
        scratch_shapes=[
            vmem((rows, d), BF16),
            vmem((3, d, hidden), BF16),
            vmem((d, 512), BF16),
            vmem((d, 896), BF16),
            vmem((3 * NB, BLK, 896), BF16),
            vmem((4, rows, 256), BF16),
            vmem((NB, 4, BLK, 256), F32),
            vmem((NB, 4, BLK, 128), F32),
            vmem((NB, 4, BLK, 128), F32),
            vmem((BLK, rows), F32),
            vmem((n_head, w_out.shape[0], d), BF16),
            vmem((d, d), BF16),
            vmem((wins, d), F32),
            vmem((n_head, wins, hidden), BF16),
            vmem((n_head, wins, hidden), BF16),
            vmem((n_head, wins, hidden), BF16),
            vmem((n_head, wins, hidden), BF16),
            vmem((rows // 2, hidden), BF16),
            vmem((rows, 128), F32),
            vmem((rows, 128), F32),
            vmem((16, 256), F32),
            dma((NB,)),
            dma((3,)),
            dma((2,)),
            dma((2, NB)),
            dma((2, NB)),
            dma((2,)),
            dma((2,)),
            dma((2,)),
            dma((2,)),
            dma((3,)),
            dma((3,)),
            dma((NB, 3)),
            dma((NB, 3)),
            dma((2, 3)),
            dma((2, 3)),
            dma((n_seq,)),
            dma((n_seq,)),
            dma((1,)),
        ],
        compiler_params=pltpu.CompilerParams(
            collective_id=0, has_side_effects=True, vmem_limit_bytes=67043328
        ),
        name="block",
    )(
        acts,
        w_qkv,
        w_out,
        gain.reshape(1, d),
        w_merge,
        seg_ids.reshape(-1, 128),
        pad_mask.reshape(-1, 128),
        owners.reshape(-1, 128),
    )


def solution(mesh):
    in_specs = (
        P("seq", None),
        P(None, None, "head"),
        P("head", None),
        P(),
        P("head", None),
        P(),
        P(),
        P("seq", None),
    )
    return jax.shard_map(
        functools.partial(per_device, mesh.shape["seq"], mesh.shape["head"]),
        mesh=mesh,
        in_specs=in_specs,
        out_specs=P("seq", "head"),
        check_vma=False,
    )
```

```python
import functools
import math

import jax
import jax.numpy as jnp
from jax import lax
from jax.experimental import pallas as pl
from jax.experimental.pallas import tpu as pltpu
from jax.sharding import PartitionSpec as P

HEAD_DIM = 104
BLK = 256
WIN = BLK // 4
NB = 4
MESH = pl.DeviceIdType.MESH
NEG = -1e30
F32 = jnp.float32
BF16 = jnp.bfloat16
K_OFF = (0, 0, 128, 256)


def iota(shape, dim):
    return lax.broadcasted_iota(jnp.int32, shape, dim)


def nt_dot(a, b):
    return lax.dot_general(a, b, (((1,), (1,)), ((), ())), preferred_element_type=F32)


def nn_dot(a, b):
    return lax.dot_general(a, b, (((1,), (0,)), ((), ())), preferred_element_type=F32)


def kernel(
    n_seq,
    n_head,
    acts_hbm,
    wqkv_hbm,
    wout_hbm,
    gain_ref,
    wmerge_hbm,
    seg_ref,
    pad_ref,
    owner_ref,
    out_hbm,
    acts,
    wq,
    wkv,
    kv,
    qm,
    acc,
    mst,
    lst,
    bias,
    wfull,
    wmerge,
    resid,
    asend,
    arecv,
    psend,
    precv,
    outgoing,
    qimg,
    qlive,
    kcode,
    acts_sem,
    wst_sem,
    wl_sem,
    kv_ssem,
    kv_rsem,
    w1_ssem,
    w1_rsem,
    w2_ssem,
    w2_rsem,
    w3_ssem,
    w3_rsem,
    a_ssem,
    a_rsem,
    p_ssem,
    p_rsem,
    o_ssem,
    o_rsem,
    o_lsem,
):
    d = acts.shape[1]
    s = lax.axis_index("seq")
    h = lax.axis_index("head")
    core = lax.rem(s, 2)
    right = lax.rem(s + 1, n_seq)
    left = lax.rem(s + n_seq - 1, n_seq)
    partner = s + 1 - 2 * core
    hp1 = lax.rem(h + 1, n_head)
    hm1 = lax.rem(h + n_head - 1, n_head)
    hp2 = lax.rem(h + 2, n_head)

    def acts_copy(c):
        rows = pl.ds(c * BLK, BLK)
        return pltpu.make_async_copy(acts_hbm.at[rows], acts.at[rows], acts_sem.at[c])

    def w_copy(n, part, src, dst, at, size):
        return pltpu.make_async_copy(
            wqkv_hbm.at[part, pl.ds(src, size)], dst.at[pl.ds(at, size)], wst_sem.at[n]
        )

    kv_loads = [
        w_copy(0, 1, 0, wkv, 0, 384),
        w_copy(1, 2, 384, wkv, 384, 32),
        w_copy(2, 1, 384, wkv, 416, 32),
        w_copy(3, 2, 0, wkv, 512, 384),
    ]
    q_loads = [w_copy(4, 0, 0, wq, 0, 384), w_copy(5, 0, 384, wq, 416, 32)]
    for copy in kv_loads:
        copy.start()
    acts_copy(3).start()
    acts_copy(0).start()
    acts_copy(2).start()
    acts_copy(1).start()
    for copy in q_loads:
        copy.start()
    wkv[448:512, :] = jnp.zeros((64, d), BF16)
    wq[384:416, :] = jnp.zeros((32, d), BF16)
    wq[448:512, :] = jnp.zeros((64, d), BF16)
    wout_local = pltpu.make_async_copy(wout_hbm, wfull.at[h], wl_sem.at[0])
    wout_local.start()
    wmerge_local = pltpu.make_async_copy(wmerge_hbm, wmerge, wl_sem.at[1])
    wmerge_local.start()

    barrier = pltpu.get_barrier_semaphore()
    for k in range(1, n_head):
        pl.semaphore_signal(
            barrier, inc=1, device_id={"head": lax.rem(h + k, n_head)}, device_id_type=MESH
        )

    def greet(k, carry):
        pl.semaphore_signal(
            barrier, inc=1, device_id={"seq": lax.rem(s + k, n_seq)}, device_id_type=MESH
        )
        return carry

    lax.fori_loop(1, n_seq, greet, 0)

    n_img_rows = seg_ref.shape[0]
    n_pad_rows = pad_ref.shape[0]
    expand = (iota((128, 512), 0) == iota((128, 512), 1) // 4).astype(BF16)
    expand_t = (iota((512, 128), 1) == iota((512, 128), 0) // 4).astype(BF16)
    eye = (iota((128, 128), 0) == iota((128, 128), 1)).astype(BF16)
    for r in range(6):
        row = 2 * s - 2 + r
        inside = jnp.logical_and(row >= 0, row < n_img_rows)
        safe = jnp.clip(row, 0, n_img_rows - 1)
        seg_row = seg_ref[pl.ds(safe, 1), :].astype(F32)
        seg_row = jnp.where(inside, seg_row, -1.0)
        wide = jnp.broadcast_to(seg_row, (128, 128)).astype(BF16)
        codes = nn_dot(wide[:16], expand)[:1]
        if 2 <= r < 4:
            qimg[(r - 2) * 512 : (r - 1) * 512, :] = nt_dot(expand_t, wide)
        for half in range(2):
            chunk = 2 * r + half if r < 2 else 2 * NB + 2 * (r - 2) + half
            if r >= 4:
                chunk = NB + 2 * (r - 4) + half
            for part in range(2):
                prow = 4 * (2 * s - 2 + r) + 2 * half + part
                pin = jnp.clip(prow, 0, n_pad_rows - 1)
                live = pad_ref[pl.ds(pin, 1), :].astype(F32)
                lanes = slice(half * 256 + part * 128, half * 256 + part * 128 + 128)
                code = jnp.where(jnp.logical_and(inside, live == 1.0), codes[:, lanes], -2.0)
                kcode[chunk : chunk + 1, part * 128 : part * 128 + 128] = code
                if 2 <= r < 4:
                    at = (r - 2) * 512 + half * 256 + part * 128
                    livew = jnp.broadcast_to(live, (128, 128)).astype(BF16)
                    qlive[at : at + 128, :] = nt_dot(eye, livew)

    for copy in kv_loads:
        copy.wait()

    pl.semaphore_wait(barrier, n_seq - 1 + n_head - 1)

    half_rows = wout_hbm.shape[0] // 2
    q_rows = (half_rows // 32 + 1) * 16
    mine = pl.ds(pl.multiple_of(core * half_rows, 16), half_rows)
    first = pl.ds(pl.multiple_of(core * half_rows, 16), q_rows)
    second = pl.ds(pl.multiple_of(core * half_rows + q_rows, 16), half_rows - q_rows)

    def remote(src, dst, ssem, rsem, dev):
        return pltpu.make_async_remote_copy(
            src_ref=src, dst_ref=dst, send_sem=ssem, recv_sem=rsem, device_id=dev, device_id_type=MESH
        )

    w1 = [
        remote(
            wout_hbm.at[mine], wfull.at[h, mine], w1_ssem.at[0], w1_rsem.at[0], {"head": hp1}
        ),
        remote(
            wout_hbm.at[mine], wfull.at[h, mine], w1_ssem.at[1], w1_rsem.at[1], {"head": hm1}
        ),
    ]
    w1[0].start()
    w1[1].start()

    def halo(t):
        way = lax.rem(t, 2)
        step = t // 2
        c = jnp.where(way == 0, NB - 1 - step, step)
        dst = jnp.where(way == 0, c, NB + c)
        to = jnp.where(way == 0, right, left)
        return c, remote(
            kv.at[2 * NB + c], kv.at[dst], kv_ssem.at[way, step], kv_rsem.at[way, step], {"seq": to}
        )

    def project_kv(t, carry):
        c, copy = halo(t)
        acts_copy(c).wait()
        rows = pl.ds(pl.multiple_of(c * BLK, BLK), BLK)
        kv[2 * NB + c] = nt_dot(acts[rows, :], wkv[...]).astype(BF16)
        copy.start()
        return carry

    lax.fori_loop(0, NB, project_kv, 0)

    def send_rest(t, carry):
        halo(t)[1].start()
        return carry

    lax.fori_loop(NB, 2 * NB, send_rest, 0)

    for copy in q_loads:
        copy.wait()
    scale = math.log2(math.e) / math.sqrt(HEAD_DIM)
    pick = (iota((WIN, BLK), 1) == 4 * iota((WIN, BLK), 0) + h).astype(BF16)

    def slot_of(i):
        return jnp.where(i == 0, 2, jnp.where(i == 3, 3, i - 1))

    def project_q(i, carry):
        rows = pl.ds(pl.multiple_of(i * BLK, BLK), BLK)
        q = nt_dot(acts[rows, :], wq[...]) * scale
        lane = iota((BLK, 512), 1)
        for k in range(4):
            lo, hi = k * HEAD_DIM, (k + 1) * HEAD_DIM if k < 3 else 512
            keep = jnp.where(jnp.logical_and(lane >= lo, lane < hi), q, 0.0)
            qm[k, rows, :] = keep[:, K_OFF[k] : K_OFF[k] + 256].astype(BF16)
        out_rows = pl.ds(pl.multiple_of(slot_of(i) * WIN, WIN), WIN)
        resid[out_rows, :] = nn_dot(pick, acts[rows, :])
        return carry

    lax.fori_loop(0, NB, project_q, 0)

    def values_of(block, k):
        if k < 3:
            off = 512 + K_OFF[k]
            return block[:, off : off + 256]
        return jnp.concatenate([block[:, 768:896], block[:, 384:512]], axis=1)

    def own(i, carry):
        rows = pl.ds(pl.multiple_of(i * BLK, BLK), BLK)
        qi = qimg[rows, :]
        qi = jnp.concatenate([qi, qi], axis=1)
        ahead = iota((BLK, BLK), 1) - iota((BLK, BLK), 0)
        for c in range(NB):
            ok = jnp.logical_or(qi == kcode[2 * NB + c : 2 * NB + c + 1, :], ahead == BLK * (i - c))
            bias[:, c * BLK : (c + 1) * BLK] = jnp.where(ok, 0.0, NEG)
        keys = kv[2 * NB : 3 * NB].reshape(NB * BLK, 896)
        for k in range(4):
            sc = nt_dot(qm[k, rows, :], keys[:, K_OFF[k] : K_OFF[k] + 256]) + bias[:, : NB * BLK]
            m = jnp.max(sc, axis=1, keepdims=True)
            p = jnp.exp2(sc - m)
            total = jnp.sum(p, axis=1, keepdims=True)
            acc[i, k] = nn_dot(p.astype(BF16), values_of(keys, k))
            mst[i, k] = jnp.broadcast_to(m, (BLK, 128))
            lst[i, k] = jnp.broadcast_to(total, (BLK, 128))
        return carry

    lax.fori_loop(0, NB, own, 0)

    w1[0].wait()
    w1[1].wait()
    w2 = [
        remote(
            wfull.at[hm1, first], wfull.at[hm1, first], w2_ssem.at[0], w2_rsem.at[0], {"head": hp1}
        ),
        remote(
            wfull.at[hp1, second], wfull.at[hp1, second], w2_ssem.at[1], w2_rsem.at[1], {"head": hm1}
        ),
    ]
    w3 = [
        remote(wfull.at[src, mine], wfull.at[src, mine], w3_ssem.at[k], w3_rsem.at[k], {"seq": partner})
        for k, src in enumerate((hm1, hp1, hp2))
    ]
    w2[0].start()
    w2[1].start()
    w3[0].start()
    w3[1].start()

    order = (iota((BLK, BLK), 1) == 4 * (iota((BLK, BLK), 0) % WIN) + iota((BLK, BLK), 0) // WIN).astype(
        BF16
    )

    def attn_copies(i):
        rows = pl.ds(pl.multiple_of(slot_of(i) * WIN, WIN), WIN)
        return [
            remote(
                asend.at[lax.rem(h + k, n_head), rows],
                arecv.at[h, rows],
                a_ssem.at[i, k - 1],
                a_rsem.at[i, k - 1],
                {"head": lax.rem(h + k, n_head)},
            )
            for k in range(1, n_head)
        ]

    def far(n, carry):
        i = jnp.where(n == 0, 1, jnp.where(n == 1, 2, jnp.where(n == 2, 0, 3)))

        def arrived(t, c2):
            halo(t)[1].wait_recv()
            return c2

        lax.fori_loop(jnp.where(n == 0, 0, NB + n), NB + 1 + n, arrived, 0)
        rows = pl.ds(pl.multiple_of(i * BLK, BLK), BLK)
        qi = qimg[rows, :]
        qi = jnp.concatenate([qi, qi], axis=1)
        for c in range(NB + 1):
            bias[:, c * BLK : (c + 1) * BLK] = jnp.where(qi == kcode[pl.ds(i + c, 1), :], 0.0, NEG)
        keys = kv[pl.ds(i, NB + 1)].reshape((NB + 1) * BLK, 896)
        live = qlive[rows, :]
        o = []
        for k in range(4):
            sc = nt_dot(qm[k, rows, :], keys[:, K_OFF[k] : K_OFF[k] + 256]) + bias[...]
            m_old = mst[i, k]
            m = jnp.maximum(m_old, jnp.max(sc, axis=1, keepdims=True))
            alpha = jnp.exp2(m_old - m)
            p = jnp.exp2(sc - m[:, :1])
            inv = live / (lst[i, k] * alpha + jnp.sum(p, axis=1, keepdims=True))
            beta = alpha * inv
            o.append(
                acc[i, k] * jnp.concatenate([beta, beta], axis=1)
                + nn_dot(p.astype(BF16), values_of(keys, k)) * jnp.concatenate([inv, inv], axis=1)
            )
        lane = iota((BLK, 128), 1)
        t0 = jnp.where(lane < HEAD_DIM, o[0][:, :128], o[1][:, :128])
        t1 = jnp.where(lane + 128 < 2 * HEAD_DIM, o[1][:, 128:], o[2][:, :128])
        t2 = jnp.where(lane + 256 < 3 * HEAD_DIM, o[2][:, 128:], o[3][:, :128])
        full = jnp.concatenate([t0, t1, t2, o[3][:, 128:]], axis=1).astype(BF16)
        sorted_rows = nn_dot(order, full).astype(BF16)
        out_rows = pl.ds(pl.multiple_of(slot_of(i) * WIN, WIN), WIN)
        for p in range(4):
            asend[p, out_rows, :] = sorted_rows[p * WIN : (p + 1) * WIN, :416]
        arecv[h, out_rows, :] = asend[h, out_rows, :]
        for copy in attn_copies(i):
            copy.start()
        return carry

    lax.fori_loop(0, 2, far, 0)
    w2[0].wait()
    w2[1].wait()
    w3[2].start()
    lax.fori_loop(2, 4, far, 0)

    wout_local.wait()
    wmerge_local.wait()
    for copy in w3:
        copy.wait()

    def part_copies(t):
        rows = pl.ds(pl.multiple_of(t * 128, 128), 128)
        return [
            remote(
                psend.at[lax.rem(h + k, n_head), rows],
                precv.at[h, rows],
                p_ssem.at[t, k - 1],
                p_rsem.at[t, k - 1],
                {"head": lax.rem(h + k, n_head)},
            )
            for k in range(1, n_head)
        ]

    def tail(t, carry):
        for i in (jnp.where(t == 0, 1, 0), jnp.where(t == 0, 2, 3)):
            for copy in attn_copies(i):
                copy.wait()
        rows = pl.ds(pl.multiple_of(t * 128, 128), 128)
        hidden = resid[rows, :]
        for src in range(4):
            hidden = hidden + nn_dot(arecv[src, rows, :], wfull[src])
        mean = jnp.sum(hidden, axis=1, keepdims=True) * (1.0 / d)
        centered = hidden - mean
        var = jnp.sum(centered * centered, axis=1, keepdims=True) * (1.0 / d)
        normed = (centered * lax.rsqrt(var + 1e-6) * gain_ref[...]).astype(BF16)
        prod = nn_dot(normed, wmerge[...])
        for c in range(4):
            psend[c, rows, :] = prod[:, c * 416 : (c + 1) * 416].astype(BF16)
        precv[h, rows, :] = psend[h, rows, :]
        for copy in part_copies(t):
            copy.start()
        return carry

    lax.fori_loop(0, 2, tail, 0)

    own0 = owner_ref[0:1, :].astype(F32)
    own1 = owner_ref[1:2, :].astype(F32)
    orow = jnp.concatenate([own0, own1], axis=1)
    ocol = jnp.concatenate(
        [
            nt_dot(eye, jnp.broadcast_to(own0, (128, 128)).astype(BF16)),
            nt_dot(eye, jnp.broadcast_to(own1, (128, 128)).astype(BF16)),
        ],
        axis=0,
    )
    ocol = jnp.concatenate([ocol, ocol], axis=1)
    earlier = jnp.logical_and(ocol == orow, iota((256, 256), 0) < iota((256, 256), 1))
    rank = jnp.sum(jnp.where(earlier, 1.0, 0.0), axis=0, keepdims=True)
    cap = 1024 // (2 * n_seq)
    slot = orow * float(cap) + rank
    place = (iota((n_seq * cap, 256), 0).astype(F32) == slot).astype(BF16)

    for t in range(2):
        for copy in part_copies(t):
            copy.wait()
    merged = (
        precv[0].astype(F32) + precv[1].astype(F32) + precv[2].astype(F32) + precv[3].astype(F32)
    ).astype(BF16)
    merged = jnp.concatenate([merged[128:192], merged[0:128], merged[192:256]], axis=0)
    outgoing[...] = nn_dot(place, merged).astype(BF16)

    def route(k):
        to = lax.rem(s + k, n_seq)
        return remote(
            outgoing.at[pl.ds(pl.multiple_of(to * cap, cap), cap)],
            out_hbm.at[pl.ds(pl.multiple_of(s * cap, cap), cap)],
            o_ssem.at[k],
            o_rsem.at[k],
            {"seq": to},
        )

    here = pl.ds(pl.multiple_of(s * cap, cap), cap)
    local = pltpu.make_async_copy(outgoing.at[here], out_hbm.at[here], o_lsem.at[0])
    local.start()

    def route_start(k, carry):
        route(k).start()
        return carry

    def route_wait(k, carry):
        route(k).wait()
        return carry

    def halo_done(t, carry):
        halo(t)[1].wait_send()
        return carry

    lax.fori_loop(1, n_seq, route_start, 0)
    lax.fori_loop(0, 2 * NB, halo_done, 0)
    lax.fori_loop(1, n_seq, route_wait, 0)
    local.wait()


def per_device(n_seq, n_head, acts, w_qkv, w_out, gain, w_merge, seg_ids, pad_mask, owners):
    rows, d = acts.shape
    hidden = w_qkv.shape[2]
    wins = rows // 4
    vmem = pltpu.VMEM
    dma = pltpu.SemaphoreType.DMA
    any_spec = pl.BlockSpec(memory_space=pl.ANY)
    vmem_spec = pl.BlockSpec(memory_space=pltpu.VMEM)
    return pl.pallas_call(
        functools.partial(kernel, n_seq, n_head),
        out_shape=jax.ShapeDtypeStruct((rows // 2, hidden), BF16),
        in_specs=[any_spec, any_spec, any_spec, vmem_spec, any_spec, vmem_spec, vmem_spec, vmem_spec],
        out_specs=any_spec,
        scratch_shapes=[
            vmem((rows, d), BF16),
            vmem((512, d), BF16),
            vmem((896, d), BF16),
            vmem((3 * NB, BLK, 896), BF16),
            vmem((4, rows, 256), BF16),
            vmem((NB, 4, BLK, 256), F32),
            vmem((NB, 4, BLK, 128), F32),
            vmem((NB, 4, BLK, 128), F32),
            vmem((BLK, (NB + 1) * BLK), F32),
            vmem((n_head, w_out.shape[0], d), BF16),
            vmem((d, d), BF16),
            vmem((wins, d), F32),
            vmem((n_head, wins, hidden), BF16),
            vmem((n_head, wins, hidden), BF16),
            vmem((n_head, wins, hidden), BF16),
            vmem((n_head, wins, hidden), BF16),
            vmem((rows // 2, hidden), BF16),
            vmem((rows, 128), F32),
            vmem((rows, 128), F32),
            vmem((16, 256), F32),
            dma((NB,)),
            dma((6,)),
            dma((2,)),
            dma((2, NB)),
            dma((2, NB)),
            dma((2,)),
            dma((2,)),
            dma((2,)),
            dma((2,)),
            dma((3,)),
            dma((3,)),
            dma((NB, 3)),
            dma((NB, 3)),
            dma((2, 3)),
            dma((2, 3)),
            dma((n_seq,)),
            dma((n_seq,)),
            dma((1,)),
        ],
        compiler_params=pltpu.CompilerParams(
            collective_id=0, has_side_effects=True, vmem_limit_bytes=67043328
        ),
        name="block",
    )(
        acts,
        jnp.swapaxes(w_qkv, 1, 2),
        w_out,
        gain,
        w_merge,
        seg_ids.reshape(-1, 128),
        pad_mask.reshape(-1, 128),
        owners.reshape(-1, 128),
    )


def solution(mesh):
    in_specs = (
        P("seq", None),
        P(None, None, "head"),
        P("head", None),
        P(),
        P("head", None),
        P(),
        P(),
        P("seq", None),
    )
    return jax.shard_map(
        functools.partial(per_device, mesh.shape["seq"], mesh.shape["head"]),
        mesh=mesh,
        in_specs=in_specs,
        out_specs=P("seq", "head"),
        check_vma=False,
    )
```

```python
import functools
import math

import jax
import jax.numpy as jnp
from jax import lax
from jax.experimental import pallas as pl
from jax.experimental.pallas import tpu as pltpu
from jax.sharding import PartitionSpec as P

HEAD_DIM = 104
BLK = 256
WIN = BLK // 4
NB = 4
MESH = pl.DeviceIdType.MESH
NEG = -1e30
F32 = jnp.float32
BF16 = jnp.bfloat16
K_OFF = (0, 0, 128, 256)


def iota(shape, dim):
    return lax.broadcasted_iota(jnp.int32, shape, dim)


def nt_dot(a, b):
    return lax.dot_general(a, b, (((1,), (1,)), ((), ())), preferred_element_type=F32)


def nn_dot(a, b):
    return lax.dot_general(a, b, (((1,), (0,)), ((), ())), preferred_element_type=F32)


def kernel(
    n_seq,
    n_head,
    acts_hbm,
    wqkv_hbm,
    wout_hbm,
    gain_ref,
    wmerge_hbm,
    seg_ref,
    pad_ref,
    owner_ref,
    out_hbm,
    acts,
    wq,
    wkv,
    kv,
    qm,
    acc,
    mst,
    lst,
    bias,
    wfull,
    wmerge,
    resid,
    asend,
    arecv,
    psend,
    precv,
    outgoing,
    qimg,
    qlive,
    kcode,
    acts_sem,
    wst_sem,
    wl_sem,
    kv_ssem,
    kv_rsem,
    w1_ssem,
    w1_rsem,
    w2_ssem,
    w2_rsem,
    w3_ssem,
    w3_rsem,
    a_ssem,
    a_rsem,
    p_ssem,
    p_rsem,
    o_ssem,
    o_rsem,
    o_lsem,
):
    d = acts.shape[1]
    s = lax.axis_index("seq")
    h = lax.axis_index("head")
    core = lax.rem(s, 2)
    right = lax.rem(s + 1, n_seq)
    left = lax.rem(s + n_seq - 1, n_seq)
    partner = s + 1 - 2 * core
    hp1 = lax.rem(h + 1, n_head)
    hm1 = lax.rem(h + n_head - 1, n_head)
    hp2 = lax.rem(h + 2, n_head)

    def acts_copy(c):
        rows = pl.ds(c * BLK, BLK)
        return pltpu.make_async_copy(acts_hbm.at[rows], acts.at[rows], acts_sem.at[c])

    def w_copy(n, part, src, dst, at, size):
        return pltpu.make_async_copy(
            wqkv_hbm.at[part, pl.ds(src, size)], dst.at[pl.ds(at, size)], wst_sem.at[n]
        )

    kv_loads = [
        w_copy(0, 1, 0, wkv, 0, 384),
        w_copy(1, 2, 384, wkv, 384, 32),
        w_copy(2, 1, 384, wkv, 416, 32),
        w_copy(3, 2, 0, wkv, 512, 384),
    ]
    q_loads = [w_copy(4, 0, 0, wq, 0, 384), w_copy(5, 0, 384, wq, 416, 32)]
    for copy in kv_loads:
        copy.start()
    acts_copy(3).start()
    acts_copy(0).start()
    acts_copy(2).start()
    acts_copy(1).start()
    for copy in q_loads:
        copy.start()
    wkv[448:512, :] = jnp.zeros((64, d), BF16)
    wq[384:416, :] = jnp.zeros((32, d), BF16)
    wq[448:512, :] = jnp.zeros((64, d), BF16)
    wout_local = pltpu.make_async_copy(wout_hbm, wfull.at[h], wl_sem.at[0])
    wout_local.start()
    wmerge_local = pltpu.make_async_copy(wmerge_hbm, wmerge, wl_sem.at[1])
    wmerge_local.start()

    barrier = pltpu.get_barrier_semaphore()
    for k in range(1, n_head):
        pl.semaphore_signal(
            barrier, inc=1, device_id={"head": lax.rem(h + k, n_head)}, device_id_type=MESH
        )

    def greet(k, carry):
        pl.semaphore_signal(
            barrier, inc=1, device_id={"seq": lax.rem(s + k, n_seq)}, device_id_type=MESH
        )
        return carry

    lax.fori_loop(1, n_seq, greet, 0)

    n_img_rows = seg_ref.shape[0]
    n_pad_rows = pad_ref.shape[0]
    expand = (iota((128, 512), 0) == iota((128, 512), 1) // 4).astype(BF16)
    expand_t = (iota((512, 128), 1) == iota((512, 128), 0) // 4).astype(BF16)
    eye = (iota((128, 128), 0) == iota((128, 128), 1)).astype(BF16)
    for r in range(6):
        row = 2 * s - 2 + r
        inside = jnp.logical_and(row >= 0, row < n_img_rows)
        safe = jnp.clip(row, 0, n_img_rows - 1)
        seg_row = seg_ref[pl.ds(safe, 1), :].astype(F32)
        seg_row = jnp.where(inside, seg_row, -1.0)
        wide = jnp.broadcast_to(seg_row, (128, 128)).astype(BF16)
        codes = nn_dot(wide[:16], expand)[:1]
        if 2 <= r < 4:
            qimg[(r - 2) * 512 : (r - 1) * 512, :] = nt_dot(expand_t, wide)
        for half in range(2):
            chunk = 2 * r + half if r < 2 else 2 * NB + 2 * (r - 2) + half
            if r >= 4:
                chunk = NB + 2 * (r - 4) + half
            for part in range(2):
                prow = 4 * (2 * s - 2 + r) + 2 * half + part
                pin = jnp.clip(prow, 0, n_pad_rows - 1)
                live = pad_ref[pl.ds(pin, 1), :].astype(F32)
                lanes = slice(half * 256 + part * 128, half * 256 + part * 128 + 128)
                code = jnp.where(jnp.logical_and(inside, live == 1.0), codes[:, lanes], -2.0)
                kcode[chunk : chunk + 1, part * 128 : part * 128 + 128] = code
                if 2 <= r < 4:
                    at = (r - 2) * 512 + half * 256 + part * 128
                    livew = jnp.broadcast_to(live, (128, 128)).astype(BF16)
                    qlive[at : at + 128, :] = nt_dot(eye, livew)

    for copy in kv_loads:
        copy.wait()

    def project_kv(c):
        acts_copy(c).wait()
        rows = pl.ds(pl.multiple_of(c * BLK, BLK), BLK)
        kv[2 * NB + c] = nt_dot(acts[rows, :], wkv[...]).astype(BF16)

    def project_first(t, carry):
        project_kv(jnp.where(t == 0, NB - 1, 0))
        return carry

    lax.fori_loop(0, 2, project_first, 0)
    pl.semaphore_wait(barrier, n_seq - 1 + n_head - 1)

    half_rows = wout_hbm.shape[0] // 2
    q_rows = (half_rows // 32 + 1) * 16
    mine = pl.ds(pl.multiple_of(core * half_rows, 16), half_rows)
    first = pl.ds(pl.multiple_of(core * half_rows, 16), q_rows)
    second = pl.ds(pl.multiple_of(core * half_rows + q_rows, 16), half_rows - q_rows)

    def remote(src, dst, ssem, rsem, dev):
        return pltpu.make_async_remote_copy(
            src_ref=src, dst_ref=dst, send_sem=ssem, recv_sem=rsem, device_id=dev, device_id_type=MESH
        )

    w1 = [
        remote(
            wout_hbm.at[mine], wfull.at[h, mine], w1_ssem.at[0], w1_rsem.at[0], {"head": hp1}
        ),
        remote(
            wout_hbm.at[mine], wfull.at[h, mine], w1_ssem.at[1], w1_rsem.at[1], {"head": hm1}
        ),
    ]
    def halo(t):
        way = lax.rem(t, 2)
        step = t // 2
        c = jnp.where(way == 0, NB - 1 - step, step)
        dst = jnp.where(way == 0, c, NB + c)
        to = jnp.where(way == 0, right, left)
        return c, remote(
            kv.at[2 * NB + c], kv.at[dst], kv_ssem.at[way, step], kv_rsem.at[way, step], {"seq": to}
        )

    halo(0)[1].start()
    halo(1)[1].start()
    w1[0].start()
    w1[1].start()

    def project_rest(t, carry):
        c, copy = halo(t)
        project_kv(c)
        copy.start()
        return carry

    lax.fori_loop(2, NB, project_rest, 0)

    def send_rest(t, carry):
        halo(t)[1].start()
        return carry

    lax.fori_loop(NB, 2 * NB, send_rest, 0)

    for copy in q_loads:
        copy.wait()
    scale = math.log2(math.e) / math.sqrt(HEAD_DIM)
    pick = (iota((WIN, BLK), 1) == 4 * iota((WIN, BLK), 0) + h).astype(BF16)

    def slot_of(i):
        return jnp.where(i == 0, 2, jnp.where(i == 3, 3, i - 1))

    def project_q(i, carry):
        rows = pl.ds(pl.multiple_of(i * BLK, BLK), BLK)
        q = nt_dot(acts[rows, :], wq[...]) * scale
        lane = iota((BLK, 512), 1)
        for k in range(4):
            lo, hi = k * HEAD_DIM, (k + 1) * HEAD_DIM if k < 3 else 512
            keep = jnp.where(jnp.logical_and(lane >= lo, lane < hi), q, 0.0)
            qm[k, rows, :] = keep[:, K_OFF[k] : K_OFF[k] + 256].astype(BF16)
        out_rows = pl.ds(pl.multiple_of(slot_of(i) * WIN, WIN), WIN)
        resid[out_rows, :] = nn_dot(pick, acts[rows, :])
        return carry

    lax.fori_loop(0, NB, project_q, 0)

    def values_of(block, k):
        if k < 3:
            off = 512 + K_OFF[k]
            return block[:, off : off + 256]
        return jnp.concatenate([block[:, 768:896], block[:, 384:512]], axis=1)

    def own(i, carry):
        rows = pl.ds(pl.multiple_of(i * BLK, BLK), BLK)
        qi = qimg[rows, :]
        qi = jnp.concatenate([qi, qi], axis=1)
        ahead = iota((BLK, BLK), 1) - iota((BLK, BLK), 0)
        for c in range(NB):
            ok = jnp.logical_or(qi == kcode[2 * NB + c : 2 * NB + c + 1, :], ahead == BLK * (i - c))
            bias[:, c * BLK : (c + 1) * BLK] = jnp.where(ok, 0.0, NEG)
        keys = kv[2 * NB : 3 * NB].reshape(NB * BLK, 896)
        for k in range(4):
            sc = nt_dot(qm[k, rows, :], keys[:, K_OFF[k] : K_OFF[k] + 256]) + bias[:, : NB * BLK]
            m = jnp.max(sc, axis=1, keepdims=True)
            p = jnp.exp2(sc - m)
            total = jnp.sum(p, axis=1, keepdims=True)
            acc[i, k] = nn_dot(p.astype(BF16), values_of(keys, k))
            mst[i, k] = jnp.broadcast_to(m, (BLK, 128))
            lst[i, k] = jnp.broadcast_to(total, (BLK, 128))
        return carry

    lax.fori_loop(0, NB, own, 0)

    w1[0].wait()
    w1[1].wait()
    w2 = [
        remote(
            wfull.at[hm1, first], wfull.at[hm1, first], w2_ssem.at[0], w2_rsem.at[0], {"head": hp1}
        ),
        remote(
            wfull.at[hp1, second], wfull.at[hp1, second], w2_ssem.at[1], w2_rsem.at[1], {"head": hm1}
        ),
    ]
    w3 = [
        remote(wfull.at[src, mine], wfull.at[src, mine], w3_ssem.at[k], w3_rsem.at[k], {"seq": partner})
        for k, src in enumerate((hm1, hp1, hp2))
    ]
    w2[0].start()
    w2[1].start()
    w3[0].start()
    w3[1].start()

    order = (iota((BLK, BLK), 1) == 4 * (iota((BLK, BLK), 0) % WIN) + iota((BLK, BLK), 0) // WIN).astype(
        BF16
    )

    def attn_copies(i):
        rows = pl.ds(pl.multiple_of(slot_of(i) * WIN, WIN), WIN)
        return [
            remote(
                asend.at[lax.rem(h + k, n_head), rows],
                arecv.at[h, rows],
                a_ssem.at[i, k - 1],
                a_rsem.at[i, k - 1],
                {"head": lax.rem(h + k, n_head)},
            )
            for k in range(1, n_head)
        ]

    def far(n, carry):
        i = jnp.where(n == 0, 1, jnp.where(n == 1, 2, jnp.where(n == 2, 0, 3)))

        def arrived(t, c2):
            halo(t)[1].wait_recv()
            return c2

        lax.fori_loop(jnp.where(n == 0, 0, NB + n), NB + 1 + n, arrived, 0)
        rows = pl.ds(pl.multiple_of(i * BLK, BLK), BLK)
        qi = qimg[rows, :]
        qi = jnp.concatenate([qi, qi], axis=1)
        for c in range(NB + 1):
            bias[:, c * BLK : (c + 1) * BLK] = jnp.where(qi == kcode[pl.ds(i + c, 1), :], 0.0, NEG)
        keys = kv[pl.ds(i, NB + 1)].reshape((NB + 1) * BLK, 896)
        live = qlive[rows, :]
        o = []
        for k in range(4):
            sc = nt_dot(qm[k, rows, :], keys[:, K_OFF[k] : K_OFF[k] + 256]) + bias[...]
            m_old = mst[i, k]
            m = jnp.maximum(m_old, jnp.max(sc, axis=1, keepdims=True))
            alpha = jnp.exp2(m_old - m)
            p = jnp.exp2(sc - m[:, :1])
            inv = live / (lst[i, k] * alpha + jnp.sum(p, axis=1, keepdims=True))
            beta = alpha * inv
            o.append(
                acc[i, k] * jnp.concatenate([beta, beta], axis=1)
                + nn_dot(p.astype(BF16), values_of(keys, k)) * jnp.concatenate([inv, inv], axis=1)
            )
        lane = iota((BLK, 128), 1)
        t0 = jnp.where(lane < HEAD_DIM, o[0][:, :128], o[1][:, :128])
        t1 = jnp.where(lane + 128 < 2 * HEAD_DIM, o[1][:, 128:], o[2][:, :128])
        t2 = jnp.where(lane + 256 < 3 * HEAD_DIM, o[2][:, 128:], o[3][:, :128])
        full = jnp.concatenate([t0, t1, t2, o[3][:, 128:]], axis=1).astype(BF16)
        sorted_rows = nn_dot(order, full).astype(BF16)
        out_rows = pl.ds(pl.multiple_of(slot_of(i) * WIN, WIN), WIN)
        for p in range(4):
            asend[p, out_rows, :] = sorted_rows[p * WIN : (p + 1) * WIN, :416]
        arecv[h, out_rows, :] = asend[h, out_rows, :]
        for copy in attn_copies(i):
            copy.start()
        return carry

    lax.fori_loop(0, 2, far, 0)
    w2[0].wait()
    w2[1].wait()
    w3[2].start()
    lax.fori_loop(2, 4, far, 0)

    wout_local.wait()
    wmerge_local.wait()
    for copy in w3:
        copy.wait()

    def part_copies(t):
        rows = pl.ds(pl.multiple_of(t * 128, 128), 128)
        return [
            remote(
                psend.at[lax.rem(h + k, n_head), rows],
                precv.at[h, rows],
                p_ssem.at[t, k - 1],
                p_rsem.at[t, k - 1],
                {"head": lax.rem(h + k, n_head)},
            )
            for k in range(1, n_head)
        ]

    def tail(t, carry):
        for i in (jnp.where(t == 0, 1, 0), jnp.where(t == 0, 2, 3)):
            for copy in attn_copies(i):
                copy.wait()
        rows = pl.ds(pl.multiple_of(t * 128, 128), 128)
        hidden = resid[rows, :]
        for src in range(4):
            hidden = hidden + nn_dot(arecv[src, rows, :], wfull[src])
        mean = jnp.sum(hidden, axis=1, keepdims=True) * (1.0 / d)
        centered = hidden - mean
        var = jnp.sum(centered * centered, axis=1, keepdims=True) * (1.0 / d)
        normed = (centered * lax.rsqrt(var + 1e-6) * gain_ref[...]).astype(BF16)
        prod = nn_dot(normed, wmerge[...])
        for c in range(4):
            psend[c, rows, :] = prod[:, c * 416 : (c + 1) * 416].astype(BF16)
        precv[h, rows, :] = psend[h, rows, :]
        for copy in part_copies(t):
            copy.start()
        return carry

    lax.fori_loop(0, 2, tail, 0)

    own0 = owner_ref[0:1, :].astype(F32)
    own1 = owner_ref[1:2, :].astype(F32)
    orow = jnp.concatenate([own0, own1], axis=1)
    ocol = jnp.concatenate(
        [
            nt_dot(eye, jnp.broadcast_to(own0, (128, 128)).astype(BF16)),
            nt_dot(eye, jnp.broadcast_to(own1, (128, 128)).astype(BF16)),
        ],
        axis=0,
    )
    ocol = jnp.concatenate([ocol, ocol], axis=1)
    earlier = jnp.logical_and(ocol == orow, iota((256, 256), 0) < iota((256, 256), 1))
    rank = jnp.sum(jnp.where(earlier, 1.0, 0.0), axis=0, keepdims=True)
    cap = 1024 // (2 * n_seq)
    slot = orow * float(cap) + rank
    place = (iota((n_seq * cap, 256), 0).astype(F32) == slot).astype(BF16)

    for t in range(2):
        for copy in part_copies(t):
            copy.wait()
    merged = (
        precv[0].astype(F32) + precv[1].astype(F32) + precv[2].astype(F32) + precv[3].astype(F32)
    ).astype(BF16)
    merged = jnp.concatenate([merged[128:192], merged[0:128], merged[192:256]], axis=0)
    outgoing[...] = nn_dot(place, merged).astype(BF16)

    def route(k):
        to = lax.rem(s + k, n_seq)
        return remote(
            outgoing.at[pl.ds(pl.multiple_of(to * cap, cap), cap)],
            out_hbm.at[pl.ds(pl.multiple_of(s * cap, cap), cap)],
            o_ssem.at[k],
            o_rsem.at[k],
            {"seq": to},
        )

    here = pl.ds(pl.multiple_of(s * cap, cap), cap)
    local = pltpu.make_async_copy(outgoing.at[here], out_hbm.at[here], o_lsem.at[0])
    local.start()

    def route_start(k, carry):
        route(k).start()
        return carry

    def route_wait(k, carry):
        route(k).wait()
        return carry

    def halo_done(t, carry):
        halo(t)[1].wait_send()
        return carry

    lax.fori_loop(1, n_seq, route_start, 0)
    lax.fori_loop(0, 2 * NB, halo_done, 0)
    lax.fori_loop(1, n_seq, route_wait, 0)
    local.wait()


def per_device(n_seq, n_head, acts, w_qkv, w_out, gain, w_merge, seg_ids, pad_mask, owners):
    rows, d = acts.shape
    hidden = w_qkv.shape[2]
    wins = rows // 4
    vmem = pltpu.VMEM
    dma = pltpu.SemaphoreType.DMA
    any_spec = pl.BlockSpec(memory_space=pl.ANY)
    vmem_spec = pl.BlockSpec(memory_space=pltpu.VMEM)
    return pl.pallas_call(
        functools.partial(kernel, n_seq, n_head),
        out_shape=jax.ShapeDtypeStruct((rows // 2, hidden), BF16),
        in_specs=[any_spec, any_spec, any_spec, vmem_spec, any_spec, vmem_spec, vmem_spec, vmem_spec],
        out_specs=any_spec,
        scratch_shapes=[
            vmem((rows, d), BF16),
            vmem((512, d), BF16),
            vmem((896, d), BF16),
            vmem((3 * NB, BLK, 896), BF16),
            vmem((4, rows, 256), BF16),
            vmem((NB, 4, BLK, 256), F32),
            vmem((NB, 4, BLK, 128), F32),
            vmem((NB, 4, BLK, 128), F32),
            vmem((BLK, (NB + 1) * BLK), F32),
            vmem((n_head, w_out.shape[0], d), BF16),
            vmem((d, d), BF16),
            vmem((wins, d), F32),
            vmem((n_head, wins, hidden), BF16),
            vmem((n_head, wins, hidden), BF16),
            vmem((n_head, wins, hidden), BF16),
            vmem((n_head, wins, hidden), BF16),
            vmem((rows // 2, hidden), BF16),
            vmem((rows, 128), F32),
            vmem((rows, 128), F32),
            vmem((16, 256), F32),
            dma((NB,)),
            dma((6,)),
            dma((2,)),
            dma((2, NB)),
            dma((2, NB)),
            dma((2,)),
            dma((2,)),
            dma((2,)),
            dma((2,)),
            dma((3,)),
            dma((3,)),
            dma((NB, 3)),
            dma((NB, 3)),
            dma((2, 3)),
            dma((2, 3)),
            dma((n_seq,)),
            dma((n_seq,)),
            dma((1,)),
        ],
        compiler_params=pltpu.CompilerParams(
            collective_id=0, has_side_effects=True, vmem_limit_bytes=67043328
        ),
        name="block",
    )(
        acts,
        jnp.swapaxes(w_qkv, 1, 2),
        w_out,
        gain,
        w_merge,
        seg_ids.reshape(-1, 128),
        pad_mask.reshape(-1, 128),
        owners.reshape(-1, 128),
    )


def solution(mesh):
    in_specs = (
        P("seq", None),
        P(None, None, "head"),
        P("head", None),
        P(),
        P("head", None),
        P(),
        P(),
        P("seq", None),
    )
    return jax.shard_map(
        functools.partial(per_device, mesh.shape["seq"], mesh.shape["head"]),
        mesh=mesh,
        in_specs=in_specs,
        out_specs=P("seq", "head"),
        check_vma=False,
    )
```

```python
import functools
import math

import jax
import jax.numpy as jnp
from jax import lax
from jax.experimental import pallas as pl
from jax.experimental.pallas import tpu as pltpu
from jax.sharding import PartitionSpec as P

HEAD_DIM = 104
BLK = 256
WIN = BLK // 4
NB = 4
MESH = pl.DeviceIdType.MESH
NEG = -1e30
F32 = jnp.float32
BF16 = jnp.bfloat16
K_OFF = (0, 0, 128, 256)


def iota(shape, dim):
    return lax.broadcasted_iota(jnp.int32, shape, dim)


def nt_dot(a, b):
    return lax.dot_general(a, b, (((1,), (1,)), ((), ())), preferred_element_type=F32)


def nn_dot(a, b):
    return lax.dot_general(a, b, (((1,), (0,)), ((), ())), preferred_element_type=F32)


def kernel(
    n_seq,
    n_head,
    acts_hbm,
    wqkv_hbm,
    wout_hbm,
    gain_ref,
    wmerge_hbm,
    seg_ref,
    pad_ref,
    owner_ref,
    out_hbm,
    acts,
    wq,
    wkv,
    kv,
    qm,
    acc,
    mst,
    lst,
    bias,
    wfull,
    wmerge,
    resid,
    asend,
    arecv,
    psend,
    precv,
    outgoing,
    qimg,
    qlive,
    kcode,
    acts_sem,
    wst_sem,
    wl_sem,
    kv_ssem,
    kv_rsem,
    w1_ssem,
    w1_rsem,
    w2_ssem,
    w2_rsem,
    w3_ssem,
    w3_rsem,
    a_ssem,
    a_rsem,
    p_ssem,
    p_rsem,
    o_ssem,
    o_rsem,
    o_lsem,
):
    d = acts.shape[1]
    s = lax.axis_index("seq")
    h = lax.axis_index("head")
    core = lax.rem(s, 2)
    right = lax.rem(s + 1, n_seq)
    left = lax.rem(s + n_seq - 1, n_seq)
    partner = s + 1 - 2 * core
    hp1 = lax.rem(h + 1, n_head)
    hm1 = lax.rem(h + n_head - 1, n_head)
    hp2 = lax.rem(h + 2, n_head)

    def acts_copy(c):
        rows = pl.ds(c * BLK, BLK)
        return pltpu.make_async_copy(acts_hbm.at[rows], acts.at[rows], acts_sem.at[c])

    def w_copy(n, part, src, dst, at, size):
        return pltpu.make_async_copy(
            wqkv_hbm.at[part, pl.ds(src, size)], dst.at[pl.ds(at, size)], wst_sem.at[n]
        )

    kv_loads = [
        w_copy(0, 1, 0, wkv, 0, 384),
        w_copy(1, 2, 384, wkv, 384, 32),
        w_copy(2, 1, 384, wkv, 416, 32),
        w_copy(3, 2, 0, wkv, 512, 384),
    ]
    q_loads = [w_copy(4, 0, 0, wq, 0, 384), w_copy(5, 0, 384, wq, 416, 32)]
    for copy in kv_loads:
        copy.start()
    acts_copy(3).start()
    acts_copy(0).start()
    acts_copy(2).start()
    acts_copy(1).start()
    for copy in q_loads:
        copy.start()
    wkv[448:512, :] = jnp.zeros((64, d), BF16)
    wq[384:416, :] = jnp.zeros((32, d), BF16)
    wq[448:512, :] = jnp.zeros((64, d), BF16)
    wout_local = pltpu.make_async_copy(wout_hbm, wfull.at[h], wl_sem.at[0])
    wout_local.start()
    wmerge_local = pltpu.make_async_copy(wmerge_hbm, wmerge, wl_sem.at[1])
    wmerge_local.start()

    barrier = pltpu.get_barrier_semaphore()
    for k in range(1, n_head):
        pl.semaphore_signal(
            barrier, inc=1, device_id={"head": lax.rem(h + k, n_head)}, device_id_type=MESH
        )

    def greet(k, carry):
        pl.semaphore_signal(
            barrier, inc=1, device_id={"seq": lax.rem(s + k, n_seq)}, device_id_type=MESH
        )
        return carry

    lax.fori_loop(1, n_seq, greet, 0)

    n_img_rows = seg_ref.shape[0]
    n_pad_rows = pad_ref.shape[0]
    expand = (iota((128, 512), 0) == iota((128, 512), 1) // 4).astype(BF16)
    expand_t = (iota((512, 128), 1) == iota((512, 128), 0) // 4).astype(BF16)
    eye = (iota((128, 128), 0) == iota((128, 128), 1)).astype(BF16)
    for r in range(6):
        row = 2 * s - 2 + r
        inside = jnp.logical_and(row >= 0, row < n_img_rows)
        safe = jnp.clip(row, 0, n_img_rows - 1)
        seg_row = seg_ref[pl.ds(safe, 1), :].astype(F32)
        seg_row = jnp.where(inside, seg_row, -1.0)
        wide = jnp.broadcast_to(seg_row, (128, 128)).astype(BF16)
        codes = nn_dot(wide[:16], expand)[:1]
        if 2 <= r < 4:
            qimg[(r - 2) * 512 : (r - 1) * 512, :] = nt_dot(expand_t, wide)
        for half in range(2):
            chunk = 2 * r + half if r < 2 else 2 * NB + 2 * (r - 2) + half
            if r >= 4:
                chunk = NB + 2 * (r - 4) + half
            for part in range(2):
                prow = 4 * (2 * s - 2 + r) + 2 * half + part
                pin = jnp.clip(prow, 0, n_pad_rows - 1)
                live = pad_ref[pl.ds(pin, 1), :].astype(F32)
                lanes = slice(half * 256 + part * 128, half * 256 + part * 128 + 128)
                code = jnp.where(jnp.logical_and(inside, live == 1.0), codes[:, lanes], -2.0)
                kcode[chunk : chunk + 1, part * 128 : part * 128 + 128] = code
                if 2 <= r < 4:
                    at = (r - 2) * 512 + half * 256 + part * 128
                    livew = jnp.broadcast_to(live, (128, 128)).astype(BF16)
                    qlive[at : at + 128, :] = nt_dot(eye, livew)

    for copy in kv_loads:
        copy.wait()

    pl.semaphore_wait(barrier, n_seq - 1 + n_head - 1)

    half_rows = wout_hbm.shape[0] // 2
    q_rows = (half_rows // 32 + 1) * 16
    mine = pl.ds(pl.multiple_of(core * half_rows, 16), half_rows)
    first = pl.ds(pl.multiple_of(core * half_rows, 16), q_rows)
    second = pl.ds(pl.multiple_of(core * half_rows + q_rows, 16), half_rows - q_rows)

    def remote(src, dst, ssem, rsem, dev):
        return pltpu.make_async_remote_copy(
            src_ref=src, dst_ref=dst, send_sem=ssem, recv_sem=rsem, device_id=dev, device_id_type=MESH
        )

    w1 = [
        remote(wout_hbm.at[part], wfull.at[h, part], w1_ssem.at[k], w1_rsem.at[k], {"head": to})
        for k, (part, to) in enumerate(((first, hp1), (second, hm1), (second, hp1), (first, hm1)))
    ]
    w1[0].start()
    w1[1].start()

    def halo(t):
        way = lax.rem(t, 2)
        step = t // 2
        c = jnp.where(way == 0, NB - 1 - step, step)
        dst = jnp.where(way == 0, c, NB + c)
        to = jnp.where(way == 0, right, left)
        return c, remote(
            kv.at[2 * NB + c], kv.at[dst], kv_ssem.at[way, step], kv_rsem.at[way, step], {"seq": to}
        )

    def project_kv(t, carry):
        c, copy = halo(t)
        acts_copy(c).wait()
        rows = pl.ds(pl.multiple_of(c * BLK, BLK), BLK)
        kv[2 * NB + c] = nt_dot(acts[rows, :], wkv[...]).astype(BF16)
        copy.start()
        return carry

    lax.fori_loop(0, NB, project_kv, 0)

    def send_rest(t, carry):
        halo(t)[1].start()
        return carry

    lax.fori_loop(NB, 2 * NB, send_rest, 0)

    for copy in q_loads:
        copy.wait()
    scale = math.log2(math.e) / math.sqrt(HEAD_DIM)
    pick = (iota((WIN, BLK), 1) == 4 * iota((WIN, BLK), 0) + h).astype(BF16)

    def slot_of(i):
        return jnp.where(i == 0, 2, jnp.where(i == 3, 3, i - 1))

    def project_q(i, carry):
        rows = pl.ds(pl.multiple_of(i * BLK, BLK), BLK)
        q = nt_dot(acts[rows, :], wq[...]) * scale
        lane = iota((BLK, 512), 1)
        for k in range(4):
            lo, hi = k * HEAD_DIM, (k + 1) * HEAD_DIM if k < 3 else 512
            keep = jnp.where(jnp.logical_and(lane >= lo, lane < hi), q, 0.0)
            qm[k, rows, :] = keep[:, K_OFF[k] : K_OFF[k] + 256].astype(BF16)
        out_rows = pl.ds(pl.multiple_of(slot_of(i) * WIN, WIN), WIN)
        resid[out_rows, :] = nn_dot(pick, acts[rows, :])
        return carry

    lax.fori_loop(0, NB, project_q, 0)
    w1[2].start()
    w1[3].start()

    def values_of(block, k):
        if k < 3:
            off = 512 + K_OFF[k]
            return block[:, off : off + 256]
        return jnp.concatenate([block[:, 768:896], block[:, 384:512]], axis=1)

    def own(i, carry):
        rows = pl.ds(pl.multiple_of(i * BLK, BLK), BLK)
        qi = qimg[rows, :]
        qi = jnp.concatenate([qi, qi], axis=1)
        ahead = iota((BLK, BLK), 1) - iota((BLK, BLK), 0)
        for c in range(NB):
            ok = jnp.logical_or(qi == kcode[2 * NB + c : 2 * NB + c + 1, :], ahead == BLK * (i - c))
            bias[:, c * BLK : (c + 1) * BLK] = jnp.where(ok, 0.0, NEG)
        keys = kv[2 * NB : 3 * NB].reshape(NB * BLK, 896)
        for k in range(4):
            sc = nt_dot(qm[k, rows, :], keys[:, K_OFF[k] : K_OFF[k] + 256]) + bias[:, : NB * BLK]
            m = jnp.max(sc, axis=1, keepdims=True)
            p = jnp.exp2(sc - m)
            total = jnp.sum(p, axis=1, keepdims=True)
            acc[i, k] = nn_dot(p.astype(BF16), values_of(keys, k))
            mst[i, k] = jnp.broadcast_to(m, (BLK, 128))
            lst[i, k] = jnp.broadcast_to(total, (BLK, 128))
        return carry

    lax.fori_loop(0, NB // 2, own, 0)

    w1[0].wait()
    w1[1].wait()
    w2 = [
        remote(
            wfull.at[hm1, first], wfull.at[hm1, first], w2_ssem.at[0], w2_rsem.at[0], {"head": hp1}
        ),
        remote(
            wfull.at[hp1, second], wfull.at[hp1, second], w2_ssem.at[1], w2_rsem.at[1], {"head": hm1}
        ),
    ]
    w3 = [
        remote(wfull.at[src, mine], wfull.at[src, mine], w3_ssem.at[k], w3_rsem.at[k], {"seq": partner})
        for k, src in enumerate((hm1, hp1, hp2))
    ]
    w2[0].start()
    w2[1].start()
    lax.fori_loop(NB // 2, NB, own, 0)
    w1[2].wait()
    w1[3].wait()
    w3[0].start()
    w3[1].start()

    order = (iota((BLK, BLK), 1) == 4 * (iota((BLK, BLK), 0) % WIN) + iota((BLK, BLK), 0) // WIN).astype(
        BF16
    )

    def attn_copies(i):
        rows = pl.ds(pl.multiple_of(slot_of(i) * WIN, WIN), WIN)
        return [
            remote(
                asend.at[lax.rem(h + k, n_head), rows],
                arecv.at[h, rows],
                a_ssem.at[i, k - 1],
                a_rsem.at[i, k - 1],
                {"head": lax.rem(h + k, n_head)},
            )
            for k in range(1, n_head)
        ]

    def far(n, carry):
        i = jnp.where(n == 0, 1, jnp.where(n == 1, 2, jnp.where(n == 2, 0, 3)))

        def arrived(t, c2):
            halo(t)[1].wait_recv()
            return c2

        lax.fori_loop(jnp.where(n == 0, 0, NB + n), NB + 1 + n, arrived, 0)
        rows = pl.ds(pl.multiple_of(i * BLK, BLK), BLK)
        qi = qimg[rows, :]
        qi = jnp.concatenate([qi, qi], axis=1)
        for c in range(NB + 1):
            bias[:, c * BLK : (c + 1) * BLK] = jnp.where(qi == kcode[pl.ds(i + c, 1), :], 0.0, NEG)
        keys = kv[pl.ds(i, NB + 1)].reshape((NB + 1) * BLK, 896)
        live = qlive[rows, :]
        o = []
        for k in range(4):
            sc = nt_dot(qm[k, rows, :], keys[:, K_OFF[k] : K_OFF[k] + 256]) + bias[...]
            m_old = mst[i, k]
            m = jnp.maximum(m_old, jnp.max(sc, axis=1, keepdims=True))
            alpha = jnp.exp2(m_old - m)
            p = jnp.exp2(sc - m[:, :1])
            inv = live / (lst[i, k] * alpha + jnp.sum(p, axis=1, keepdims=True))
            beta = alpha * inv
            o.append(
                acc[i, k] * jnp.concatenate([beta, beta], axis=1)
                + nn_dot(p.astype(BF16), values_of(keys, k)) * jnp.concatenate([inv, inv], axis=1)
            )
        lane = iota((BLK, 128), 1)
        t0 = jnp.where(lane < HEAD_DIM, o[0][:, :128], o[1][:, :128])
        t1 = jnp.where(lane + 128 < 2 * HEAD_DIM, o[1][:, 128:], o[2][:, :128])
        t2 = jnp.where(lane + 256 < 3 * HEAD_DIM, o[2][:, 128:], o[3][:, :128])
        full = jnp.concatenate([t0, t1, t2, o[3][:, 128:]], axis=1).astype(BF16)
        sorted_rows = nn_dot(order, full).astype(BF16)
        out_rows = pl.ds(pl.multiple_of(slot_of(i) * WIN, WIN), WIN)
        for p in range(4):
            asend[p, out_rows, :] = sorted_rows[p * WIN : (p + 1) * WIN, :416]
        arecv[h, out_rows, :] = asend[h, out_rows, :]
        for copy in attn_copies(i):
            copy.start()
        return carry

    lax.fori_loop(0, 2, far, 0)
    w2[0].wait()
    w2[1].wait()
    w3[2].start()
    lax.fori_loop(2, 4, far, 0)

    wout_local.wait()
    wmerge_local.wait()
    for copy in w3:
        copy.wait()

    def part_copies(t):
        rows = pl.ds(pl.multiple_of(t * 128, 128), 128)
        return [
            remote(
                psend.at[lax.rem(h + k, n_head), rows],
                precv.at[h, rows],
                p_ssem.at[t, k - 1],
                p_rsem.at[t, k - 1],
                {"head": lax.rem(h + k, n_head)},
            )
            for k in range(1, n_head)
        ]

    def tail(t, carry):
        for i in (jnp.where(t == 0, 1, 0), jnp.where(t == 0, 2, 3)):
            for copy in attn_copies(i):
                copy.wait()
        rows = pl.ds(pl.multiple_of(t * 128, 128), 128)
        hidden = resid[rows, :]
        for src in range(4):
            hidden = hidden + nn_dot(arecv[src, rows, :], wfull[src])
        mean = jnp.sum(hidden, axis=1, keepdims=True) * (1.0 / d)
        centered = hidden - mean
        var = jnp.sum(centered * centered, axis=1, keepdims=True) * (1.0 / d)
        normed = (centered * lax.rsqrt(var + 1e-6) * gain_ref[...]).astype(BF16)
        prod = nn_dot(normed, wmerge[...])
        for c in range(4):
            psend[c, rows, :] = prod[:, c * 416 : (c + 1) * 416].astype(BF16)
        precv[h, rows, :] = psend[h, rows, :]
        for copy in part_copies(t):
            copy.start()
        return carry

    lax.fori_loop(0, 2, tail, 0)

    own0 = owner_ref[0:1, :].astype(F32)
    own1 = owner_ref[1:2, :].astype(F32)
    orow = jnp.concatenate([own0, own1], axis=1)
    ocol = jnp.concatenate(
        [
            nt_dot(eye, jnp.broadcast_to(own0, (128, 128)).astype(BF16)),
            nt_dot(eye, jnp.broadcast_to(own1, (128, 128)).astype(BF16)),
        ],
        axis=0,
    )
    ocol = jnp.concatenate([ocol, ocol], axis=1)
    earlier = jnp.logical_and(ocol == orow, iota((256, 256), 0) < iota((256, 256), 1))
    rank = jnp.sum(jnp.where(earlier, 1.0, 0.0), axis=0, keepdims=True)
    cap = 1024 // (2 * n_seq)
    slot = orow * float(cap) + rank
    place = (iota((n_seq * cap, 256), 0).astype(F32) == slot).astype(BF16)

    for t in range(2):
        for copy in part_copies(t):
            copy.wait()
    merged = (
        precv[0].astype(F32) + precv[1].astype(F32) + precv[2].astype(F32) + precv[3].astype(F32)
    ).astype(BF16)
    merged = jnp.concatenate([merged[128:192], merged[0:128], merged[192:256]], axis=0)
    outgoing[...] = nn_dot(place, merged).astype(BF16)

    def route(k):
        to = lax.rem(s + k, n_seq)
        return remote(
            outgoing.at[pl.ds(pl.multiple_of(to * cap, cap), cap)],
            out_hbm.at[pl.ds(pl.multiple_of(s * cap, cap), cap)],
            o_ssem.at[k],
            o_rsem.at[k],
            {"seq": to},
        )

    here = pl.ds(pl.multiple_of(s * cap, cap), cap)
    local = pltpu.make_async_copy(outgoing.at[here], out_hbm.at[here], o_lsem.at[0])
    local.start()

    def route_start(k, carry):
        route(k).start()
        return carry

    def route_wait(k, carry):
        route(k).wait()
        return carry

    def halo_done(t, carry):
        halo(t)[1].wait_send()
        return carry

    lax.fori_loop(1, n_seq, route_start, 0)
    lax.fori_loop(0, 2 * NB, halo_done, 0)
    lax.fori_loop(1, n_seq, route_wait, 0)
    local.wait()


def per_device(n_seq, n_head, acts, w_qkv, w_out, gain, w_merge, seg_ids, pad_mask, owners):
    rows, d = acts.shape
    hidden = w_qkv.shape[2]
    wins = rows // 4
    vmem = pltpu.VMEM
    dma = pltpu.SemaphoreType.DMA
    any_spec = pl.BlockSpec(memory_space=pl.ANY)
    vmem_spec = pl.BlockSpec(memory_space=pltpu.VMEM)
    return pl.pallas_call(
        functools.partial(kernel, n_seq, n_head),
        out_shape=jax.ShapeDtypeStruct((rows // 2, hidden), BF16),
        in_specs=[any_spec, any_spec, any_spec, vmem_spec, any_spec, vmem_spec, vmem_spec, vmem_spec],
        out_specs=any_spec,
        scratch_shapes=[
            vmem((rows, d), BF16),
            vmem((512, d), BF16),
            vmem((896, d), BF16),
            vmem((3 * NB, BLK, 896), BF16),
            vmem((4, rows, 256), BF16),
            vmem((NB, 4, BLK, 256), F32),
            vmem((NB, 4, BLK, 128), F32),
            vmem((NB, 4, BLK, 128), F32),
            vmem((BLK, (NB + 1) * BLK), F32),
            vmem((n_head, w_out.shape[0], d), BF16),
            vmem((d, d), BF16),
            vmem((wins, d), F32),
            vmem((n_head, wins, hidden), BF16),
            vmem((n_head, wins, hidden), BF16),
            vmem((n_head, wins, hidden), BF16),
            vmem((n_head, wins, hidden), BF16),
            vmem((rows // 2, hidden), BF16),
            vmem((rows, 128), F32),
            vmem((rows, 128), F32),
            vmem((16, 256), F32),
            dma((NB,)),
            dma((6,)),
            dma((2,)),
            dma((2, NB)),
            dma((2, NB)),
            dma((4,)),
            dma((4,)),
            dma((2,)),
            dma((2,)),
            dma((3,)),
            dma((3,)),
            dma((NB, 3)),
            dma((NB, 3)),
            dma((2, 3)),
            dma((2, 3)),
            dma((n_seq,)),
            dma((n_seq,)),
            dma((1,)),
        ],
        compiler_params=pltpu.CompilerParams(
            collective_id=0, has_side_effects=True, vmem_limit_bytes=67043328
        ),
        name="block",
    )(
        acts,
        jnp.swapaxes(w_qkv, 1, 2),
        w_out,
        gain,
        w_merge,
        seg_ids.reshape(-1, 128),
        pad_mask.reshape(-1, 128),
        owners.reshape(-1, 128),
    )


def solution(mesh):
    in_specs = (
        P("seq", None),
        P(None, None, "head"),
        P("head", None),
        P(),
        P("head", None),
        P(),
        P(),
        P("seq", None),
    )
    return jax.shard_map(
        functools.partial(per_device, mesh.shape["seq"], mesh.shape["head"]),
        mesh=mesh,
        in_specs=in_specs,
        out_specs=P("seq", "head"),
        check_vma=False,
    )
```
